32 devices in a mesh: parts: 1, row: 16 (over z, y, x), chan: 1, sub: 2 (over core).
Axes of the slice: x: 2, y: 2, z: 4, core: 2. Of those that a mesh axis runs over, the one named last changes fastest.
Arguments:
- pair: bfloat16 [448, 448, 128], P(('parts', 'row', 'sub'), 'chan'), may hold values from -6 to 6
- pair_mask: int32 [448, 448], P(('parts', 'row', 'sub'), 'chan'), may hold values 0 or 1
- out_in_gain: float32 [128], replicated, may hold values from 0.5 to 1.5
- out_proj: bfloat16 [128, 640], replicated, may hold values from -0.5 to 0.5
- out_mid_gain: float32 [128], replicated, may hold values from 0.5 to 1.5
- out_final: bfloat16 [128, 128], replicated, may hold values from -0.5 to 0.5
- in_in_gain: float32 [128], replicated, may hold values from 0.5 to 1.5
- in_proj: bfloat16 [128, 640], replicated, may hold values from -0.5 to 0.5
- in_mid_gain: float32 [128], replicated, may hold values from 0.5 to 1.5
- in_final: bfloat16 [128, 128], replicated, may hold values from -0.5 to 0.5
Outputs:
- updated: bfloat16 [448, 448, 128], P(('parts', 'row', 'sub'), 'chan')
The draws below stay inside these ranges and needn't reach their ends.
All inputs are finite; a program needn't handle non-finite values. No bound on the sum of `pair_mask` on one device may be relied on, other than what follows from the above.
Results may differ from the reference program's by a relative error of at most 0.014.
Values may be sent and summed in bfloat16 or wider, within the bound.
A program may use at most 192 MiB of HBM per device.

```python
import jax
import jax.numpy as jnp
from jax import lax

CHANNELS = 128
HIDDEN_SIZE = 128
TOKENS = 448


def place_ends(values, own_key, least, high):
    longest = values.shape.index(max(values.shape))
    spots = []
    for shift in (0, 1):
        where = [jax.random.randint(jax.random.fold_in(own_key, axis), (), 0, length) for axis, length in enumerate(values.shape)]
        where[longest] = (where[longest] + shift) % values.shape[longest]
        spots.append(tuple(where))
    return values.at[spots[0]].set(least).at[spots[1]].set(high)


def level_of(stream_key, shape, shards, low, top_value):
    def one(axis_at, blocks):
        heights = jax.random.uniform(jax.random.fold_in(jax.random.fold_in(stream_key, 6), axis_at), (blocks,), jnp.float32, low / len(shards), top_value / len(shards))
        return jnp.repeat(jnp.exp(heights), shape[axis_at] // blocks).reshape((-1,) + (1,) * (len(shape) - axis_at - 1))

    loudness = one(*shards[0])
    for cut in shards[1:]:
        loudness = loudness * one(*cut)
    return loudness


def normal_values(stream_key, shape, spread, reach, shards=(), dtype=jnp.bfloat16):
    level = level_of(stream_key, shape, shards, -0.22, 0.18) if shards else 1.0
    entries = jax.random.normal(stream_key, shape, jnp.float32) * spread * level
    return jnp.minimum(jnp.maximum(entries, -reach), reach).astype(dtype)


def setup_inputs(seed: int = 0, part: int = 0) -> dict:
    key_of = jax.random.split(jax.random.key(seed), 11)
    own_keys = jax.random.split(jax.random.fold_in(key_of[10], part), 11)
    return {
        "pair": normal_values(own_keys[0], (TOKENS, TOKENS, CHANNELS), 1.0, 6.0, ((0, 32),)),
        "pair_mask": place_ends((jax.random.randint(own_keys[1], (TOKENS, TOKENS), 0, 4) < 3).astype(jnp.int32), jax.random.fold_in(own_keys[1], 1), 0, 1),
        "out_in_gain": jnp.clip(jax.random.uniform(key_of[2], (CHANNELS,), jnp.float32, 0.5, 1.5), 0.5, 1.5),
        "out_proj": normal_values(key_of[3], (CHANNELS, 4 * HIDDEN_SIZE + CHANNELS), CHANNELS ** -0.5, 0.5),
        "out_mid_gain": jnp.clip(jax.random.uniform(key_of[4], (HIDDEN_SIZE,), jnp.float32, 0.5, 1.5), 0.5, 1.5),
        "out_final": normal_values(key_of[5], (HIDDEN_SIZE, CHANNELS), HIDDEN_SIZE ** -0.5, 0.5),
        "in_in_gain": jnp.clip(jax.random.uniform(key_of[6], (CHANNELS,), jnp.float32, 0.5, 1.5), 0.5, 1.5),
        "in_proj": normal_values(key_of[7], (CHANNELS, 4 * HIDDEN_SIZE + CHANNELS), CHANNELS ** -0.5, 0.5),
        "in_mid_gain": jnp.clip(jax.random.uniform(key_of[8], (HIDDEN_SIZE,), jnp.float32, 0.5, 1.5), 0.5, 1.5),
        "in_final": normal_values(key_of[9], (HIDDEN_SIZE, CHANNELS), HIDDEN_SIZE ** -0.5, 0.5),
    }


def norm_last(values, gain):
    mean = lax.optimization_barrier(jnp.mean(values, axis=-1, keepdims=True))
    var = lax.optimization_barrier(jnp.mean((values - mean) ** 2, axis=-1, keepdims=True))
    return (values - mean) / jnp.sqrt(var + 1e-05) * gain

def triangle(pair, pair_mask, in_gain, proj, mid_gain, final, incoming):
    normed = norm_last(pair.astype(jnp.float32), in_gain).astype(jnp.bfloat16)
    slabs = jnp.dot(normed, proj[:, :4 * HIDDEN_SIZE], preferred_element_type=jnp.float32)
    keep = pair_mask.astype(jnp.float32)[:, :, None]
    left = (jax.nn.sigmoid(slabs[:, :, :HIDDEN_SIZE]) * slabs[:, :, HIDDEN_SIZE:2 * HIDDEN_SIZE] * keep).astype(jnp.bfloat16)
    right = (jax.nn.sigmoid(slabs[:, :, 2 * HIDDEN_SIZE:3 * HIDDEN_SIZE]) * slabs[:, :, 3 * HIDDEN_SIZE:] * keep).astype(jnp.bfloat16)
    gate = jax.nn.sigmoid(jnp.dot(normed, proj[:, 4 * HIDDEN_SIZE:], preferred_element_type=jnp.float32))
    left_c = jnp.moveaxis(left, 2, 0).astype(jnp.float32)
    right_c = jnp.moveaxis(right, 2, 0).astype(jnp.float32)
    if incoming:
        prod = jnp.einsum('cki,ckj->cij', left_c, right_c)
    else:
        prod = jnp.einsum('cik,cjk->cij', left_c, right_c)
    normed_mid = norm_last(jnp.moveaxis(prod, 0, 2), mid_gain).astype(jnp.bfloat16)
    update = gate * jnp.dot(normed_mid, final, preferred_element_type=jnp.float32)
    return (pair.astype(jnp.float32) + update).astype(jnp.bfloat16)

def reference(pair, pair_mask, out_in_gain, out_proj, out_mid_gain, out_final, in_in_gain, in_proj, in_mid_gain, in_final):
    middle = triangle(pair, pair_mask, out_in_gain, out_proj, out_mid_gain, out_final, False)
    return triangle(middle, pair_mask, in_in_gain, in_proj, in_mid_gain, in_final, True)
```

```python
import functools

import jax
import jax.numpy as jnp
from jax import lax
from jax.experimental import pallas as pl
from jax.experimental.pallas import tpu as pltpu
from jax.sharding import PartitionSpec as P

AXES = ("row", "sub")


def place(index, subs):
    return {"row": index // subs, "sub": index % subs}


def spread_order(count):
    stride = next((step for step in (11, 7, 5, 3) if count % step), 1)
    return [(step * stride) % count for step in range(1, count)]


def exchange_kernel(count, subs, halves, routes, *refs):
    kinds = len(routes)
    sources, targets = refs[:kinds], refs[kinds : 2 * kinds]
    send_sem, recv_sem, local_sem = refs[2 * kinds :]
    me = lax.axis_index("row") * subs + lax.axis_index("sub")
    groups = count // halves
    my_half, my_group = me // groups, me % groups

    def block(kind, half, group):
        return sources[kind].at[half, group] if routes[kind] == "split" else sources[kind].at[group]

    def slot(kind, half, group):
        return targets[kind].at[group] if routes[kind] == "own" else targets[kind].at[half * groups + group]

    barrier = pltpu.get_barrier_semaphore()
    others = range(1, groups) if all(route == "own" for route in routes) else range(1, count)
    for step in others:
        if len(others) == groups - 1:
            other = my_half * groups + (my_group + step) % groups
        else:
            other = (me + step) % count
        pl.semaphore_signal(barrier, inc=1, device_id=place(other, subs))
    pl.semaphore_wait(barrier, len(others))

    plan = []
    for shift_half in range(halves - 1, -1, -1):
        for shift in [*spread_order(groups), 0]:
            for kind in range(kinds):
                if shift_half and routes[kind] == "own":
                    continue
                plan.append((kind, shift_half, shift))

    sent = []
    for number, (kind, shift_half, shift) in enumerate(plan):
        half, group = (my_half + shift_half) % halves, (my_group + shift) % groups
        if shift_half == 0 and shift == 0:
            copy = pltpu.make_async_copy(
                block(kind, my_half, my_group), slot(kind, my_half, my_group), local_sem.at[kind]
            )
        else:
            copy = pltpu.make_async_remote_copy(
                src_ref=block(kind, half, group),
                dst_ref=slot(kind, my_half, my_group),
                send_sem=send_sem.at[number],
                recv_sem=recv_sem.at[number],
                device_id=place(half * groups + group, subs),
            )
        copy.start()
        sent.append(copy)
    for number, (kind, shift_half, shift) in enumerate(plan):
        if shift_half == 0 and shift == 0:
            sent[number].wait()
            continue
        half, group = (
            (my_half + halves - shift_half) % halves,
            (my_group + groups - shift) % groups,
        )
        sent[number].wait_send()
        pltpu.make_async_remote_copy(
            src_ref=block(kind, half, group),
            dst_ref=slot(kind, half, group),
            send_sem=send_sem.at[number],
            recv_sem=recv_sem.at[number],
            device_id=place(half * groups + group, subs),
        ).wait_recv()


def exchange(operands, routes, halves, collective_id):
    count = lax.axis_size("row") * lax.axis_size("sub")
    subs = lax.axis_size("sub")
    groups = count // halves
    shapes = []
    for operand, route in zip(operands, routes):
        tail = operand.shape[2:] if route == "split" else operand.shape[1:]
        shapes.append(
            jax.ShapeDtypeStruct((groups if route == "own" else count, *tail), operand.dtype)
        )
    copies = count * len(operands)
    return pl.pallas_call(
        functools.partial(exchange_kernel, count, subs, halves, routes),
        out_shape=shapes,
        in_specs=[pl.BlockSpec(memory_space=pl.ANY)] * len(operands),
        out_specs=[pl.BlockSpec(memory_space=pl.ANY)] * len(operands),
        scratch_shapes=[
            pltpu.SemaphoreType.DMA((copies,)),
            pltpu.SemaphoreType.DMA((copies,)),
            pltpu.SemaphoreType.DMA((len(operands),)),
        ],
        compiler_params=pltpu.CompilerParams(collective_id=collective_id, has_side_effects=True),
        name=f"exchange_{collective_id}",
    )(*operands)


def flat_project(pair, pair_mask, in_gain, proj, halves):
    rows, columns, channels = pair.shape
    hidden = (proj.shape[1] - channels) // 4
    normed = norm_last(pair.astype(jnp.float32), in_gain).astype(jnp.bfloat16)
    keep = pair_mask.astype(jnp.float32)
    right_raw = jnp.einsum(
        "pd,de->ep",
        normed.reshape(rows * columns, channels),
        proj[:, 2 * hidden : 4 * hidden],
        preferred_element_type=jnp.float32,
    )
    right = (
        jax.nn.sigmoid(right_raw[:hidden]) * right_raw[hidden:] * keep.reshape(1, -1)
    ).astype(jnp.bfloat16)
    parted = normed.reshape(rows, halves, columns // halves, channels).transpose(1, 0, 2, 3)
    parted_keep = keep.reshape(rows, halves, columns // halves).transpose(1, 0, 2)
    left_raw = jnp.einsum(
        "hpd,de->hep",
        parted.reshape(halves, -1, channels),
        proj[:, : 2 * hidden],
        preferred_element_type=jnp.float32,
    )
    left = (
        jax.nn.sigmoid(left_raw[:, :hidden])
        * left_raw[:, hidden:]
        * parted_keep.reshape(halves, 1, -1)
    ).astype(jnp.bfloat16)
    gate = jax.nn.sigmoid(
        jnp.dot(normed, proj[:, 4 * hidden :], preferred_element_type=jnp.float32)
    )
    return left, right, gate


def flat_finish(pair, product, gate, mid_gain, final):
    values = product.astype(jnp.float32)
    mean = jnp.mean(values, axis=0, keepdims=True)
    var = jnp.mean((values - mean) ** 2, axis=0, keepdims=True)
    normed = ((values - mean) / jnp.sqrt(var + 1e-05) * mid_gain[:, None]).astype(jnp.bfloat16)
    update = jnp.einsum("cp,cd->pd", normed, final, preferred_element_type=jnp.float32)
    return (pair.astype(jnp.float32) + gate * update.reshape(gate.shape)).astype(jnp.bfloat16)


def whole_rows(received, columns):
    sources, width, area = received.shape
    parts = received.reshape(sources, width, area // columns, columns)
    return parts.transpose(1, 0, 2, 3).reshape(width, -1, columns)


def back(product, groups, halves, rows, columns, mid_id):
    width = product.shape[0]
    blocks = product.astype(jnp.bfloat16).reshape(width, groups, rows, columns)
    blocks = blocks.transpose(1, 0, 2, 3).reshape(groups, width, rows * columns)
    (received,) = exchange((blocks,), ("own",), halves, mid_id)
    return received.reshape(groups * width, rows * columns)


def grouped_shards(
    pair,
    pair_mask,
    out_in_gain,
    out_proj,
    out_mid_gain,
    out_final,
    in_in_gain,
    in_proj,
    in_mid_gain,
    in_final,
):
    rows, columns, channels = pair.shape
    hidden = (out_proj.shape[1] - channels) // 4
    count = lax.axis_size("row") * lax.axis_size("sub")
    halves = halves_of(count)
    groups = count // halves
    width = hidden // groups

    left, right, gate = flat_project(pair, pair_mask, out_in_gain, out_proj, 1)
    left, right = exchange(
        (left.reshape(groups, width, -1), right.reshape(groups, width, -1)),
        ("own", "all"),
        halves,
        0,
    )
    product = jnp.einsum(
        "cik,cjk->cij",
        whole_rows(left, columns),
        whole_rows(right, columns),
        preferred_element_type=jnp.float32,
    )
    received = back(product, groups, halves, rows, columns, 1)
    middle = flat_finish(pair, received, gate, out_mid_gain, out_final)

    left, right, gate = flat_project(middle, pair_mask, in_in_gain, in_proj, halves)
    left, right = exchange(
        (left.reshape(halves, groups, width, -1), right.reshape(groups, width, -1)),
        ("split", "all"),
        halves,
        2,
    )
    product = jnp.einsum(
        "cki,ckj->cij",
        whole_rows(left, columns // halves),
        whole_rows(right, columns),
        preferred_element_type=jnp.float32,
    )
    received = back(product, groups, halves, rows, columns, 3)
    return flat_finish(middle, received, gate, in_mid_gain, in_final)


def halves_of(count):
    return 2 if count % 2 == 0 else 1


def norm_last(values, gain):
    mean = jnp.mean(values, axis=-1, keepdims=True)
    var = jnp.mean((values - mean) ** 2, axis=-1, keepdims=True)
    return (values - mean) / jnp.sqrt(var + 1e-05) * gain


def project(pair, pair_mask, in_gain, proj, left_form, right_form, left_across):
    hidden = (proj.shape[1] - pair.shape[2]) // 4
    normed = norm_last(pair.astype(jnp.float32), in_gain).astype(jnp.bfloat16)
    keep = pair_mask.astype(jnp.float32)
    left_raw = jnp.einsum(
        left_form, normed, proj[:, : 2 * hidden], preferred_element_type=jnp.float32
    )
    right_raw = jnp.einsum(
        right_form, normed, proj[:, 2 * hidden : 4 * hidden], preferred_element_type=jnp.float32
    )
    left_keep = keep.T[None] if left_across else keep[None]
    left = (jax.nn.sigmoid(left_raw[:hidden]) * left_raw[hidden:] * left_keep).astype(jnp.bfloat16)
    right = (jax.nn.sigmoid(right_raw[:hidden]) * right_raw[hidden:] * keep[None]).astype(
        jnp.bfloat16
    )
    gate = jax.nn.sigmoid(
        jnp.dot(normed, proj[:, 4 * hidden :], preferred_element_type=jnp.float32)
    )
    return (left, right, gate)


def finish(pair, product, gate, mid_gain, final):
    group = product.shape[0]
    total = group * lax.axis_size("chan")
    first, second = (
        lax.psum(jnp.sum(product, axis=0).astype(jnp.bfloat16), "chan").astype(jnp.float32),
        lax.psum(jnp.sum(product * product, axis=0).astype(jnp.bfloat16), "chan").astype(
            jnp.float32
        ),
    )
    mean = first / total
    var = second / total - mean * mean
    offset = lax.axis_index("chan") * group
    gain_part = lax.dynamic_slice_in_dim(mid_gain, offset, group, 0)
    final_part = lax.dynamic_slice_in_dim(final, offset, group, 0)
    normed = ((product - mean) / jnp.sqrt(var + 1e-05) * gain_part[:, None, None]).astype(
        jnp.bfloat16
    )
    summed = lax.psum_scatter(
        jnp.einsum("crj,cd->jrd", normed, final_part, preferred_element_type=jnp.float32).astype(
            jnp.bfloat16
        ),
        "chan",
        scatter_dimension=0,
        tiled=True,
    ).astype(jnp.float32)
    update = jnp.transpose(summed, (1, 0, 2))
    return (pair.astype(jnp.float32) + gate * update).astype(jnp.bfloat16)


def shards(
    pair,
    pair_mask,
    out_in_gain,
    out_proj,
    out_mid_gain,
    out_final,
    in_in_gain,
    in_proj,
    in_mid_gain,
    in_final,
):
    left, right, gate = project(
        pair, pair_mask, out_in_gain, out_proj, "rqd,de->erq", "rqd,de->erq", False
    )
    left, right = (
        lax.all_to_all(left, "chan", split_axis=0, concat_axis=2, tiled=True),
        lax.all_to_all(right, "chan", split_axis=0, concat_axis=2, tiled=True),
    )
    product = jnp.einsum(
        "cik,cjk->cij",
        left,
        lax.all_gather(right, ("row", "sub"), axis=1, tiled=True),
        preferred_element_type=jnp.float32,
    )
    middle = finish(pair, product, gate, out_mid_gain, out_final)
    left_in, right_in, gate_in = project(
        middle, pair_mask, in_in_gain, in_proj, "rqd,de->eqr", "rqd,de->erq", True
    )
    columns = lax.all_to_all(
        lax.all_to_all(left_in, "chan", split_axis=0, concat_axis=1, tiled=True),
        ("row", "sub"),
        split_axis=1,
        concat_axis=2,
        tiled=True,
    )
    right_in = lax.all_to_all(right_in, "chan", split_axis=0, concat_axis=2, tiled=True)
    product_in = jnp.einsum(
        "cik,ckj->cij",
        columns,
        lax.all_gather(right_in, ("row", "sub"), axis=1, tiled=True),
        preferred_element_type=jnp.float32,
    )
    return finish(middle, product_in, gate_in, in_mid_gain, in_final)


def solution(mesh):
    placed = (
        P(("parts", "row", "sub"), "chan", None),
        P(("parts", "row", "sub"), "chan"),
        P(),
        P(),
        P(),
        P(),
        P(),
        P(),
        P(),
        P(),
    )
    sizes = mesh.shape
    return jax.shard_map(
        grouped_shards if sizes["chan"] == 1 and sizes["parts"] == 1 else shards,
        mesh=mesh,
        in_specs=placed,
        out_specs=P(("parts", "row", "sub"), "chan", None),
        check_vma=False,
    )
```

```python
import functools

import jax
import jax.numpy as jnp
from jax import lax
from jax.experimental import pallas as pl
from jax.experimental.pallas import tpu as pltpu
from jax.sharding import PartitionSpec as P

AXES = ("row", "sub")


def place(index, subs):
    return {"row": index // subs, "sub": index % subs}


def spread_order(count):
    stride = next((step for step in (11, 7, 5, 3) if count % step), 1)
    return [(step * stride) % count for step in range(1, count)]


def exchange_kernel(count, subs, halves, routes, *refs):
    kinds = len(routes)
    sources, targets = refs[:kinds], refs[kinds : 2 * kinds]
    send_sem, recv_sem, local_sem = refs[2 * kinds :]
    me = lax.axis_index("row") * subs + lax.axis_index("sub")
    groups = count // halves
    my_half, my_group = me // groups, me % groups

    def block(kind, group):
        return sources[kind].at[group]

    def slot(kind, half, group):
        return targets[kind].at[group] if routes[kind] == "own" else targets[kind].at[half * groups + group]

    barrier = pltpu.get_barrier_semaphore()
    others = range(1, groups) if all(route == "own" for route in routes) else range(1, count)
    for step in others:
        if len(others) == groups - 1:
            other = my_half * groups + (my_group + step) % groups
        else:
            other = (me + step) % count
        pl.semaphore_signal(barrier, inc=1, device_id=place(other, subs))
    pl.semaphore_wait(barrier, len(others))

    plan = []
    for shift_half in range(halves - 1, -1, -1):
        for shift in [*spread_order(groups), 0]:
            for kind in range(kinds):
                if shift_half and routes[kind] == "own":
                    continue
                plan.append((kind, shift_half, shift))

    sent = []
    for number, (kind, shift_half, shift) in enumerate(plan):
        half, group = (my_half + shift_half) % halves, (my_group + shift) % groups
        if shift_half == 0 and shift == 0:
            copy = pltpu.make_async_copy(
                block(kind, my_group), slot(kind, my_half, my_group), local_sem.at[kind]
            )
        else:
            copy = pltpu.make_async_remote_copy(
                src_ref=block(kind, group),
                dst_ref=slot(kind, my_half, my_group),
                send_sem=send_sem.at[number],
                recv_sem=recv_sem.at[number],
                device_id=place(half * groups + group, subs),
            )
        copy.start()
        sent.append(copy)
    for number, (kind, shift_half, shift) in enumerate(plan):
        if shift_half == 0 and shift == 0:
            sent[number].wait()
            continue
        half, group = (
            (my_half + halves - shift_half) % halves,
            (my_group + groups - shift) % groups,
        )
        sent[number].wait_send()
        pltpu.make_async_remote_copy(
            src_ref=block(kind, group),
            dst_ref=slot(kind, half, group),
            send_sem=send_sem.at[number],
            recv_sem=recv_sem.at[number],
            device_id=place(half * groups + group, subs),
        ).wait_recv()


def exchange(operands, routes, halves, collective_id):
    count = lax.axis_size("row") * lax.axis_size("sub")
    subs = lax.axis_size("sub")
    groups = count // halves
    shapes = []
    for operand, route in zip(operands, routes):
        shapes.append(
            jax.ShapeDtypeStruct((groups if route == "own" else count, *operand.shape[1:]), operand.dtype)
        )
    copies = count * len(operands)
    return pl.pallas_call(
        functools.partial(exchange_kernel, count, subs, halves, routes),
        out_shape=shapes,
        in_specs=[pl.BlockSpec(memory_space=pl.ANY)] * len(operands),
        out_specs=[pl.BlockSpec(memory_space=pl.ANY)] * len(operands),
        scratch_shapes=[
            pltpu.SemaphoreType.DMA((copies,)),
            pltpu.SemaphoreType.DMA((copies,)),
            pltpu.SemaphoreType.DMA((len(operands),)),
        ],
        compiler_params=pltpu.CompilerParams(collective_id=collective_id, has_side_effects=True),
        name=f"exchange_{collective_id}",
    )(*operands)


def flat_project(pair, pair_mask, in_gain, proj):
    rows, columns, channels = pair.shape
    hidden = (proj.shape[1] - channels) // 4
    normed = norm_last(pair.astype(jnp.float32), in_gain).astype(jnp.bfloat16)
    keep = pair_mask.astype(jnp.float32).reshape(1, -1)
    raw = jnp.einsum(
        "pd,de->ep",
        normed.reshape(rows * columns, channels),
        proj[:, : 4 * hidden],
        preferred_element_type=jnp.float32,
    )
    parts = raw.reshape(4, hidden, rows * columns)
    left = (jax.nn.sigmoid(parts[0]) * parts[1] * keep).astype(jnp.bfloat16)
    right = (jax.nn.sigmoid(parts[2]) * parts[3] * keep).astype(jnp.bfloat16)
    gate = jax.nn.sigmoid(
        jnp.dot(normed, proj[:, 4 * hidden :], preferred_element_type=jnp.float32)
    )
    return left, right, gate


def flat_finish(pair, product, gate, mid_gain, final):
    values = product.astype(jnp.float32)
    mean = jnp.mean(values, axis=0, keepdims=True)
    var = jnp.mean((values - mean) ** 2, axis=0, keepdims=True)
    normed = ((values - mean) / jnp.sqrt(var + 1e-05) * mid_gain[:, None]).astype(jnp.bfloat16)
    update = jnp.einsum("cp,cd->pd", normed, final, preferred_element_type=jnp.float32)
    return (pair.astype(jnp.float32) + gate * update.reshape(gate.shape)).astype(jnp.bfloat16)


def whole_rows(received, columns):
    sources, width, area = received.shape
    parts = received.reshape(sources, width, area // columns, columns)
    return parts.transpose(1, 0, 2, 3).reshape(width, -1, columns)


def back(product, groups, halves, rows, columns, mid_id):
    width = product.shape[0]
    blocks = product.astype(jnp.bfloat16).reshape(width, groups, rows, columns)
    blocks = blocks.transpose(1, 0, 2, 3).reshape(groups, width, rows * columns)
    (received,) = exchange((blocks,), ("own",), halves, mid_id)
    return received.reshape(groups * width, rows * columns)


def grouped_shards(
    pair,
    pair_mask,
    out_in_gain,
    out_proj,
    out_mid_gain,
    out_final,
    in_in_gain,
    in_proj,
    in_mid_gain,
    in_final,
):
    rows, columns, channels = pair.shape
    hidden = (out_proj.shape[1] - channels) // 4
    count = lax.axis_size("row") * lax.axis_size("sub")
    halves = halves_of(count)
    groups = count // halves
    width = hidden // groups

    left, right, gate = flat_project(pair, pair_mask, out_in_gain, out_proj)
    left, right = exchange(
        (left.reshape(groups, width, -1), right.reshape(groups, width, -1)),
        ("own", "all"),
        halves,
        0,
    )
    product = jnp.einsum(
        "cik,cjk->cij",
        whole_rows(left, columns),
        whole_rows(right, columns),
        preferred_element_type=jnp.float32,
    )
    received = back(product, groups, halves, rows, columns, 1)
    middle = flat_finish(pair, received, gate, out_mid_gain, out_final)

    groups, width = count, hidden // count
    left, right, gate = flat_project(middle, pair_mask, in_in_gain, in_proj)
    left, right = exchange(
        (left.reshape(groups, width, -1), right.reshape(groups, width, -1)),
        ("own", "own"),
        1,
        2,
    )
    product = jnp.einsum(
        "cki,ckj->cij",
        whole_rows(left, columns),
        whole_rows(right, columns),
        preferred_element_type=jnp.float32,
    )
    received = back(product, groups, 1, rows, columns, 3)
    return flat_finish(middle, received, gate, in_mid_gain, in_final)


def halves_of(count):
    return 2 if count % 2 == 0 else 1


def norm_last(values, gain):
    mean = jnp.mean(values, axis=-1, keepdims=True)
    var = jnp.mean((values - mean) ** 2, axis=-1, keepdims=True)
    return (values - mean) / jnp.sqrt(var + 1e-05) * gain


def project(pair, pair_mask, in_gain, proj, left_form, right_form, left_across):
    hidden = (proj.shape[1] - pair.shape[2]) // 4
    normed = norm_last(pair.astype(jnp.float32), in_gain).astype(jnp.bfloat16)
    keep = pair_mask.astype(jnp.float32)
    left_raw = jnp.einsum(
        left_form, normed, proj[:, : 2 * hidden], preferred_element_type=jnp.float32
    )
    right_raw = jnp.einsum(
        right_form, normed, proj[:, 2 * hidden : 4 * hidden], preferred_element_type=jnp.float32
    )
    left_keep = keep.T[None] if left_across else keep[None]
    left = (jax.nn.sigmoid(left_raw[:hidden]) * left_raw[hidden:] * left_keep).astype(jnp.bfloat16)
    right = (jax.nn.sigmoid(right_raw[:hidden]) * right_raw[hidden:] * keep[None]).astype(
        jnp.bfloat16
    )
    gate = jax.nn.sigmoid(
        jnp.dot(normed, proj[:, 4 * hidden :], preferred_element_type=jnp.float32)
    )
    return (left, right, gate)


def finish(pair, product, gate, mid_gain, final):
    group = product.shape[0]
    total = group * lax.axis_size("chan")
    first, second = (
        lax.psum(jnp.sum(product, axis=0).astype(jnp.bfloat16), "chan").astype(jnp.float32),
        lax.psum(jnp.sum(product * product, axis=0).astype(jnp.bfloat16), "chan").astype(
            jnp.float32
        ),
    )
    mean = first / total
    var = second / total - mean * mean
    offset = lax.axis_index("chan") * group
    gain_part = lax.dynamic_slice_in_dim(mid_gain, offset, group, 0)
    final_part = lax.dynamic_slice_in_dim(final, offset, group, 0)
    normed = ((product - mean) / jnp.sqrt(var + 1e-05) * gain_part[:, None, None]).astype(
        jnp.bfloat16
    )
    summed = lax.psum_scatter(
        jnp.einsum("crj,cd->jrd", normed, final_part, preferred_element_type=jnp.float32).astype(
            jnp.bfloat16
        ),
        "chan",
        scatter_dimension=0,
        tiled=True,
    ).astype(jnp.float32)
    update = jnp.transpose(summed, (1, 0, 2))
    return (pair.astype(jnp.float32) + gate * update).astype(jnp.bfloat16)


def shards(
    pair,
    pair_mask,
    out_in_gain,
    out_proj,
    out_mid_gain,
    out_final,
    in_in_gain,
    in_proj,
    in_mid_gain,
    in_final,
):
    left, right, gate = project(
        pair, pair_mask, out_in_gain, out_proj, "rqd,de->erq", "rqd,de->erq", False
    )
    left, right = (
        lax.all_to_all(left, "chan", split_axis=0, concat_axis=2, tiled=True),
        lax.all_to_all(right, "chan", split_axis=0, concat_axis=2, tiled=True),
    )
    product = jnp.einsum(
        "cik,cjk->cij",
        left,
        lax.all_gather(right, ("row", "sub"), axis=1, tiled=True),
        preferred_element_type=jnp.float32,
    )
    middle = finish(pair, product, gate, out_mid_gain, out_final)
    left_in, right_in, gate_in = project(
        middle, pair_mask, in_in_gain, in_proj, "rqd,de->eqr", "rqd,de->erq", True
    )
    columns = lax.all_to_all(
        lax.all_to_all(left_in, "chan", split_axis=0, concat_axis=1, tiled=True),
        ("row", "sub"),
        split_axis=1,
        concat_axis=2,
        tiled=True,
    )
    right_in = lax.all_to_all(right_in, "chan", split_axis=0, concat_axis=2, tiled=True)
    product_in = jnp.einsum(
        "cik,ckj->cij",
        columns,
        lax.all_gather(right_in, ("row", "sub"), axis=1, tiled=True),
        preferred_element_type=jnp.float32,
    )
    return finish(middle, product_in, gate_in, in_mid_gain, in_final)


def solution(mesh):
    placed = (
        P(("parts", "row", "sub"), "chan", None),
        P(("parts", "row", "sub"), "chan"),
        P(),
        P(),
        P(),
        P(),
        P(),
        P(),
        P(),
        P(),
    )
    sizes = mesh.shape
    return jax.shard_map(
        grouped_shards if sizes["chan"] == 1 and sizes["parts"] == 1 else shards,
        mesh=mesh,
        in_specs=placed,
        out_specs=P(("parts", "row", "sub"), "chan", None),
        check_vma=False,
    )
```
